32 devices in a mesh: parts: 2 (over y), bank: 8 (over z, x), batch: 2 (over core).
Axes of the slice: x: 2, y: 2, z: 4, core: 2. Of those that a mesh axis runs over, the one named last changes fastest.
Arguments:
- bank: bfloat16 [32768, 256], P(('parts', 'bank')), parts along dimension 0, may hold values from -1 to 1
- queries: bfloat16 [4096, 256], P(('parts', 'batch')), parts along dimension 0, may hold values from -8 to 8
- keys: bfloat16 [4096, 256], P(('parts', 'batch')), parts along dimension 0, may hold values from -0.375 to 0.375
- labels: int32 [4096], P(('parts', 'batch')), parts along dimension 0, may hold values from 0 to 2047, each once
- mask_tiles: int32 [32, 16], P('parts'), parts along dimension 0, may hold values from 0 to 127
Outputs:
- new_bank: bfloat16 [32768, 256], P(('parts', 'bank')), parts along dimension 0
- query_grad: float32 [4096, 256], P(('parts', 'batch')), parts along dimension 0
- loss: float32 [4096], P(('parts', 'batch')), parts along dimension 0
The draws below stay inside these ranges and needn't reach their ends.
There are 2 independent parts, one for each index of `parts`. The reference program is written for one: setup_inputs(seed, part) draws one part's arguments, and reference() takes and returns one part's arrays. A program takes and returns all parts, laid end to end along the dimension named above; each array names one. Nothing has to cross between parts.
Inputs may be any that keep to these rules, and one draw needn't show every extreme that they name: `labels`: a permutation: each row of keys is the positive of exactly one query. `mask_tiles`: tile t holds bank rows t * 128 to t * 128 + 127; row b lists tiles excluded for queries b * 128 to b * 128 + 127; numbers may repeat.
All inputs are finite; a program needn't handle non-finite values.
Results may differ from the reference program's by a relative error of at most 0.0055.
Values may be sent and summed in bfloat16 or wider, within the bound.
A program may use at most 64 MiB of HBM per device.

```python
import math
import jax
import jax.numpy as jnp
from jax import lax

D = 256
TILE = 128
BANK = 16384
QUERIES = 2048
QBLK = 16
KT = 128
MB = 16


def draw_bank(key, part):
    k_base = jax.random.fold_in(jax.random.fold_in(key, 1), 0)
    ramp = 0.75 + 0.5 * jnp.arange(BANK, dtype=jnp.float32) / BANK
    base = jax.random.truncated_normal(k_base, -6.0, 6.0, (BANK, D), jnp.float32) * ramp[:, None] * D ** (-0.5)
    return base.astype(jnp.bfloat16)


def draw_queries(key, part):
    k_base = jax.random.fold_in(jax.random.fold_in(key, 2), 0)
    base = 0.35 * jax.random.truncated_normal(k_base, -6.0, 6.0, (QUERIES, D), jnp.float32)
    return base.astype(jnp.bfloat16)


def touch_ends(array, key, smallest, largest):
    longest = array.shape.index(max(array.shape))
    spots = []
    for shift in (0, 1):
        where = [jax.random.randint(jax.random.fold_in(key, axis), (), 0, length) for axis, length in enumerate(array.shape)]
        where[longest] = (where[longest] + shift) % array.shape[longest]
        spots.append(tuple(where))
    return array.at[spots[0]].set(smallest).at[spots[1]].set(largest)


def level_of(own_key, shape, cuts, smallest, largest):
    gain, own = 1.0, jax.random.fold_in(own_key, 6)
    for dim, parts in cuts:
        steps = jnp.exp(jax.random.uniform(jax.random.fold_in(own, dim), (parts,), jnp.float32, smallest / len(cuts), largest / len(cuts)))
        gain = gain * jnp.repeat(steps, shape[dim] // parts).reshape([-1 if axis == dim else 1 for axis in range(len(shape))])
    return gain


def noise(own_key, extent, deviation, most, cuts=(), kind=jnp.bfloat16):
    level = level_of(own_key, extent, cuts, -0.22, 0.18) if cuts else 1.0
    result = jax.random.normal(own_key, extent, jnp.float32) * deviation * level
    return jnp.minimum(jnp.maximum(result, -most), most).astype(kind)


def setup_inputs(seed: int = 0, part: int = 0) -> dict:
    arg_keys = jax.random.split(jax.random.key(seed), 6)
    part_splits = jax.random.split(jax.random.fold_in(arg_keys[5], part), 6)
    bank = draw_bank(jax.random.fold_in(jax.random.fold_in(arg_keys[5], part), 71), part)
    queries = draw_queries(jax.random.fold_in(jax.random.fold_in(arg_keys[5], part), 71), part)
    keys = noise(part_splits[2], (QUERIES, D), (D ** -0.5), 0.375, ((0, 2),))
    labels = jax.random.permutation(part_splits[3], QUERIES).astype(jnp.int32)
    mask_tiles = touch_ends(jax.random.randint(part_splits[4], (QBLK, MB), 0, KT), jax.random.fold_in(part_splits[4], 1), 0, KT - 1).astype(jnp.int32)
    return dict(bank=bank, queries=queries, keys=keys, labels=labels, mask_tiles=mask_tiles)


TAU = 0.12
NEG = -1e+30
EPS = 1e-06

def masked_scores(rows_q, rows_k, mask_rows, first):
    s = jnp.dot(rows_q, rows_k.T, preferred_element_type=jnp.float32) / TAU
    nq, nk = s.shape
    ids = (first + jnp.arange(nk // TILE, dtype=jnp.int32)).astype(jnp.int32)
    hit = jnp.any(mask_rows[:, :, None] == ids[None, None, :], axis=1)
    live = jnp.broadcast_to(jnp.logical_not(hit)[:, None, :, None], (nq // TILE, TILE, nk // TILE, TILE)).reshape(nq, nk)
    return (jnp.where(live, s, NEG), live)

def reference(bank, queries, keys, labels, mask_tiles):
    block = math.gcd(BANK, 16384)
    count = BANK // block
    eta = 0.25 * BANK / QUERIES
    key_rows = keys[labels]
    pos = lax.optimization_barrier(jnp.sum(queries.astype(jnp.float32) * key_rows.astype(jnp.float32), axis=1)) / TAU
    groups = bank.reshape(count, block, D)
    starts = (jnp.arange(count, dtype=jnp.int32) * (block // TILE)).astype(jnp.int32)

    def stats(carry, item):
        top, total = carry
        rows, first = item
        s, live = masked_scores(queries, rows, mask_tiles, first)
        cmax = lax.optimization_barrier(jnp.max(s, axis=1))
        csum = lax.optimization_barrier(jnp.sum(jnp.where(live, jnp.exp(s - cmax[:, None]), 0.0), axis=1))
        high = jnp.maximum(top, cmax)
        return ((high, total * jnp.exp(top - high) + csum * jnp.exp(cmax - high)), None)
    init = (jnp.full((QUERIES,), NEG, jnp.float32), jnp.zeros((QUERIES,), jnp.float32))
    (top, total), unused = lax.scan(stats, init, (groups, starts))
    high = jnp.maximum(top, pos)
    lse = high + jnp.log(total * jnp.exp(top - high) + jnp.exp(pos - high))
    loss = lse - pos

    def grads(neg, item):
        rows, first = item
        s, live = masked_scores(queries, rows, mask_tiles, first)
        probs = jnp.exp(s - lse[:, None]).astype(jnp.bfloat16)
        neg = neg + jnp.dot(probs, rows, preferred_element_type=jnp.float32)
        pull = jnp.dot(probs.T, queries, preferred_element_type=jnp.float32)
        fresh = rows.astype(jnp.float32) + eta * pull
        fresh = fresh * lax.rsqrt(lax.optimization_barrier(jnp.mean(fresh * fresh, axis=1, keepdims=True)) + EPS)
        return (neg, fresh.astype(jnp.bfloat16))
    neg, fresh = lax.scan(grads, jnp.zeros((QUERIES, D), jnp.float32), (groups, starts))
    query_grad = (neg + (jnp.exp(pos - lse) - 1.0)[:, None] * key_rows.astype(jnp.float32)) / TAU
    return (fresh.reshape(BANK, D), query_grad, loss)
```

```python
import functools
import math

import jax
import jax.numpy as jnp
from jax import lax
from jax.experimental import pallas as pl
from jax.experimental.pallas import tpu as pltpu
from jax.sharding import PartitionSpec as P

TILE = 128


TAU = 0.12
NEG = -1e30
FLOOR = -1e29
EPS = 1e-06
LOG2E = math.log2(math.e)
LN2 = math.log(2.0)
SCALE2 = LOG2E / TAU
QCH = 256
BCH = 256
MESH = pl.DeviceIdType.MESH


def masked_scores(rows_q, rows_k, mask_rows, first):
    s = jnp.einsum("qd,kd->qk", rows_q, rows_k, preferred_element_type=jnp.float32) / TAU
    nq, nk = s.shape
    ids = first + jnp.arange(nk // TILE, dtype=jnp.int32)
    hit = jnp.any(mask_rows[:, :, None] == ids[None, None, :], axis=1)
    live = jnp.broadcast_to(
        jnp.logical_not(hit)[:, None, :, None], (nq // TILE, TILE, nk // TILE, TILE)
    ).reshape(nq, nk)
    return (jnp.where(live, s, NEG), live)


def general(bank, queries, keys, labels, mask_tiles):
    qdev = queries.shape[0]
    bdev = bank.shape[0]
    total_bank = bdev * lax.axis_size("bank")
    total_query = qdev * lax.axis_size("batch")
    eta = 0.25 * total_bank / total_query
    mine = lax.axis_index("batch")
    first = lax.axis_index("bank") * (bdev // TILE)
    all_keys = lax.all_gather(keys, "batch", axis=0, tiled=True)
    key_rows = jnp.take(all_keys, labels, axis=0)
    pos = jnp.sum(queries.astype(jnp.float32) * key_rows.astype(jnp.float32), axis=1) / TAU
    own_mask = lax.dynamic_slice_in_dim(mask_tiles, mine * (qdev // TILE), qdev // TILE, 0)
    scores, live = masked_scores(queries, bank, own_mask, first)
    top = lax.pmax(jnp.max(scores, axis=1), "bank")
    part_sum = jnp.sum(jnp.where(live, jnp.exp(scores - top[:, None]), 0.0), axis=1)
    total = lax.psum(part_sum, "bank")
    high = jnp.maximum(top, pos)
    lse = high + jnp.log(total * jnp.exp(top - high) + jnp.exp(pos - high))
    loss = lse - pos
    probs = jnp.exp(scores - lse[:, None]).astype(jnp.bfloat16)
    neg_local = jnp.dot(probs, bank, preferred_element_type=jnp.float32)
    own_pull = jnp.einsum("qk,qd->kd", probs, queries, preferred_element_type=jnp.float32)
    neg = lax.psum(neg_local, "bank")
    query_grad = (neg + (jnp.exp(pos - lse) - 1.0)[:, None] * key_rows.astype(jnp.float32)) / TAU
    pull = lax.psum(own_pull.astype(jnp.bfloat16), "batch").astype(jnp.float32)
    fresh = bank.astype(jnp.float32) + eta * pull
    fresh = fresh * lax.rsqrt(jnp.mean(fresh * fresh, axis=1, keepdims=True) + EPS)
    return (fresh.astype(jnp.bfloat16), query_grad, loss)


def column(row):
    return jnp.transpose(jnp.broadcast_to(row, (TILE, TILE)))


def wide_column(row, width):
    return jnp.concatenate([column(row)] * (width // TILE), axis=1)


def step_kernel(
    n, eta, mask_ref, bank_ref, q_ref, keys_ref, labels_ref,
    new_ref, grad_ref, loss_ref,
    s_scr, p_scr, bankt_scr, bias_scr, neg_scr, keys_scr, stats_scr, qs_scr,
    stage_scr, rs_scr, pull_scr, pull_in_scr,
    keys_sems, stats_send, stats_recv, rs_send, rs_recv, ag_send, ag_recv, pull_send, pull_recv,
):
    me = lax.axis_index("bank")
    mine = lax.axis_index("batch")
    other = 1 - mine
    bdev, width = bank_ref.shape
    qdev = q_ref.shape[0]
    tiles = bdev // TILE
    blocks = qdev // TILE
    listed = mask_ref.shape[1]
    first = me * tiles

    barrier = pltpu.get_barrier_semaphore()
    for d in range(1, n):
        pl.semaphore_signal(barrier, inc=1, device_id={"bank": lax.rem(me + d, n)}, device_id_type=MESH)
    pl.semaphore_signal(barrier, inc=1, device_id={"batch": other}, device_id_type=MESH)

    ids = first + lax.broadcasted_iota(jnp.int32, (tiles, TILE), 0)
    for b in range(blocks):
        hit = ids == mask_ref[mine * blocks + b, 0]
        for m in range(1, listed):
            hit = jnp.logical_or(hit, ids == mask_ref[mine * blocks + b, m])
        bias_scr[:, b * TILE:(b + 1) * TILE] = jnp.where(hit, NEG, 0.0)

    for k in range(bdev // BCH):
        bankt_scr[:, k * BCH:(k + 1) * BCH] = jnp.transpose(bank_ref[k * BCH:(k + 1) * BCH, :])

    def keys_copy():
        return pltpu.make_async_remote_copy(
            src_ref=keys_ref, dst_ref=keys_scr, send_sem=keys_sems.at[0], recv_sem=keys_sems.at[1],
            device_id={"batch": other}, device_id_type=MESH)

    for c in range(qdev // QCH):
        cols = slice(c * QCH, (c + 1) * QCH)
        qc = q_ref[cols, :]
        top8 = jnp.full((8, QCH), FLOOR, jnp.float32)
        for k in range(bdev // BCH):
            s = lax.dot_general(bank_ref[k * BCH:(k + 1) * BCH, :], qc, (((1,), (1,)), ((), ())),
                                preferred_element_type=jnp.float32)
            for t in range(BCH // TILE):
                tile = k * (BCH // TILE) + t
                part = s[t * TILE:(t + 1) * TILE, :] * SCALE2 + bias_scr[tile:tile + 1, cols]
                s_scr[c % 2, tile * TILE:(tile + 1) * TILE, :] = part
                top8 = jnp.maximum(top8, jnp.max(part.reshape(TILE // 8, 8, QCH), axis=0))
        top = jnp.max(top8, axis=0, keepdims=True)
        sum8 = jnp.zeros((8, QCH), jnp.float32)
        for tile in range(tiles):
            rows = slice(tile * TILE, (tile + 1) * TILE)
            p = jnp.exp2(s_scr[c % 2, rows, :] - top)
            sum8 = sum8 + jnp.sum(p.reshape(TILE // 8, 8, QCH), axis=0)
            p_scr[rows, cols] = p.astype(jnp.bfloat16)
        total = jnp.sum(sum8, axis=0, keepdims=True)
        for t in range(QCH // TILE):
            b = c * (QCH // TILE) + t
            stats_scr[me, b:b + 1, :] = top[:, t * TILE:(t + 1) * TILE]
            stats_scr[me, 8 + b:9 + b, :] = total[:, t * TILE:(t + 1) * TILE]
        if c == 0:
            pl.semaphore_wait(barrier, n)
            keys_copy().start()

    own = pl.ds(pl.multiple_of(me * TILE, TILE), TILE)
    label_row = labels_ref[pl.ds(me, 1), :]
    row_ids = lax.broadcasted_iota(jnp.int32, (qdev, TILE), 0)

    def picked(table, start):
        hot = jnp.where(row_ids + start == label_row, 1.0, 0.0).astype(jnp.bfloat16)
        return lax.dot_general(hot, table, (((0,), (0,)), ((), ())), preferred_element_type=jnp.float32)

    key_rows = picked(keys_ref[...], mine * qdev)
    keys_copy().wait()
    key_rows = key_rows + picked(keys_scr[...], other * qdev)
    prod = q_ref[own, :].astype(jnp.float32) * key_rows
    own_pos = jnp.sum(jnp.transpose(prod), axis=0, keepdims=True) / TAU
    stats_scr[me, 16:24, :] = jnp.broadcast_to(own_pos, (8, TILE))

    def to_peer(d, src, dst, send, recv):
        return pltpu.make_async_remote_copy(
            src_ref=src, dst_ref=dst, send_sem=send.at[d], recv_sem=recv.at[d],
            device_id={"bank": lax.rem(me + d, n)}, device_id_type=MESH)

    stats = [to_peer(d, stats_scr.at[me], stats_scr.at[me], stats_send, stats_recv) for d in range(1, n)]
    for copy in stats:
        copy.start()

    for c in range(qdev // QCH):
        cols = slice(c * QCH, (c + 1) * QCH)
        neg_scr[:, cols] = jnp.dot(bankt_scr[...], p_scr[:, cols], preferred_element_type=jnp.float32)

    for copy in stats:
        copy.wait()
    high = jnp.concatenate([stats_scr[b, 16:17, :] for b in range(n)], axis=0) * LOG2E
    pos = high
    for b in range(n):
        high = jnp.maximum(high, stats_scr[b, 0:8, :])
    total = jnp.exp2(pos - high)
    for b in range(n):
        total = total + stats_scr[b, 8:16, :] * jnp.exp2(stats_scr[b, 0:8, :] - high)
    lse = high + jnp.log(total) * LOG2E
    loss_ref[...] = (lse - pos) * LN2
    alpha = jnp.exp2(stats_scr[me, 0:8, :] - lse)

    for b in range(blocks):
        stage_scr[b] = (neg_scr[:, b * TILE:(b + 1) * TILE] * alpha[b:b + 1, :]).astype(jnp.bfloat16)
    scatter = []
    for d in range(1, n):
        copy = to_peer(d, stage_scr.at[lax.rem(me + d, n)], rs_scr.at[d], rs_send, rs_recv)
        copy.start()
        scatter.append(copy)

    for b in range(blocks):
        rows = slice(b * TILE, (b + 1) * TILE)
        qs_scr[rows, :] = (q_ref[rows, :].astype(jnp.float32) * wide_column(alpha[b:b + 1, :], width)).astype(jnp.bfloat16)
    exchange = []
    for k in range(bdev // BCH):
        rows = slice(k * BCH, (k + 1) * BCH)
        pull_scr[rows, :] = jnp.dot(p_scr[rows, :], qs_scr[...], preferred_element_type=jnp.float32).astype(jnp.bfloat16)
        copy = pltpu.make_async_remote_copy(
            src_ref=pull_scr.at[rows, :], dst_ref=pull_in_scr.at[rows, :],
            send_sem=pull_send.at[k], recv_sem=pull_recv.at[k],
            device_id={"batch": other}, device_id_type=MESH)
        copy.start()
        exchange.append(copy)

    row_of = lax.broadcasted_iota(jnp.int32, (n, TILE), 0) == me
    factor = jnp.sum(jnp.where(row_of, jnp.exp2(pos - lse) - 1.0, 0.0), axis=0, keepdims=True)
    negs = stage_scr[me].astype(jnp.float32)
    for d in range(1, n):
        scatter[d - 1].wait()
        negs = negs + rs_scr[d].astype(jnp.float32)
    grad = (jnp.transpose(negs) + wide_column(factor, width) * key_rows) / TAU
    grad_ref[me] = grad.astype(jnp.bfloat16)
    gather = []
    for d in range(1, n):
        copy = to_peer(d, grad_ref.at[me], grad_ref.at[me], ag_send, ag_recv)
        copy.start()
        gather.append(copy)

    for k in range(bdev // BCH):
        rows = slice(k * BCH, (k + 1) * BCH)
        exchange[k].wait()
        pull = pull_scr[rows, :].astype(jnp.float32) + pull_in_scr[rows, :].astype(jnp.float32)
        fresh = bank_ref[rows, :].astype(jnp.float32) + eta * pull
        fresh = fresh * lax.rsqrt(jnp.mean(fresh * fresh, axis=1, keepdims=True) + EPS)
        new_ref[rows, :] = fresh.astype(jnp.bfloat16)
    for copy in gather:
        copy.wait()


def fused(bank, queries, keys, labels, mask_tiles):
    n = lax.axis_size("bank")
    qdev, width = queries.shape
    bdev = bank.shape[0]
    eta = 0.25 * (bdev * n) / (qdev * lax.axis_size("batch"))
    vmem = pl.BlockSpec(memory_space=pltpu.VMEM)
    dma = pltpu.SemaphoreType.DMA
    new_bank, grad, loss = pl.pallas_call(
        functools.partial(step_kernel, n, eta),
        out_shape=(
            jax.ShapeDtypeStruct((bdev, width), jnp.bfloat16),
            jax.ShapeDtypeStruct((n, TILE, width), jnp.bfloat16),
            jax.ShapeDtypeStruct((n, TILE), jnp.float32),
        ),
        in_specs=[pl.BlockSpec(memory_space=pltpu.SMEM)] + [vmem] * 4,
        out_specs=(vmem, vmem, vmem),
        scratch_shapes=[
            pltpu.VMEM((2, bdev, QCH), jnp.float32),
            pltpu.VMEM((bdev, qdev), jnp.bfloat16),
            pltpu.VMEM((width, bdev), jnp.bfloat16),
            pltpu.VMEM((bdev // TILE, qdev), jnp.float32),
            pltpu.VMEM((width, qdev), jnp.float32),
            pltpu.VMEM((qdev, width), jnp.bfloat16),
            pltpu.VMEM((n, 24, TILE), jnp.float32),
            pltpu.VMEM((qdev, width), jnp.bfloat16),
            pltpu.VMEM((n, width, TILE), jnp.bfloat16),
            pltpu.VMEM((n, width, TILE), jnp.bfloat16),
            pltpu.VMEM((bdev, width), jnp.bfloat16),
            pltpu.VMEM((bdev, width), jnp.bfloat16),
            dma((2,)),
            dma((n,)), dma((n,)),
            dma((n,)), dma((n,)),
            dma((n,)), dma((n,)),
            dma((bdev // BCH,)), dma((bdev // BCH,)),
        ],
        compiler_params=pltpu.CompilerParams(
            collective_id=0, has_side_effects=True, vmem_limit_bytes=48 * 1024 * 1024
        ),
    )(mask_tiles, bank, queries, keys, labels.reshape(n, TILE))
    return (new_bank, grad.reshape(qdev, width).astype(jnp.float32), loss.reshape(qdev))


def on_device(bank, queries, keys, labels, mask_tiles):
    n = lax.axis_size("bank")
    fits = (
        n == 8
        and queries.shape[0] == n * TILE
        and bank.shape[0] % BCH == 0
        and lax.axis_size("batch") == 2
    )
    return (fused if fits else general)(bank, queries, keys, labels, mask_tiles)


def solution(mesh):
    return jax.shard_map(
        on_device,
        mesh=mesh,
        in_specs=(
            P(("parts", "bank"), None),
            P(("parts", "batch"), None),
            P(("parts", "batch"), None),
            P(("parts", "batch")),
            P("parts", None),
        ),
        out_specs=(P(("parts", "bank"), None), P(("parts", "batch"), None), P(("parts", "batch"))),
        check_vma=False,
    )
```

```python
import functools
import math

import jax
import jax.numpy as jnp
from jax import lax
from jax.experimental import pallas as pl
from jax.experimental.pallas import tpu as pltpu
from jax.sharding import PartitionSpec as P

TILE = 128


TAU = 0.12
NEG = -1e30
FLOOR = -1e29
EPS = 1e-06
LOG2E = math.log2(math.e)
LN2 = math.log(2.0)
SCALE2 = LOG2E / TAU
QCH = 256
BCH = 256
MESH = pl.DeviceIdType.MESH


def masked_scores(rows_q, rows_k, mask_rows, first):
    s = jnp.einsum("qd,kd->qk", rows_q, rows_k, preferred_element_type=jnp.float32) / TAU
    nq, nk = s.shape
    ids = first + jnp.arange(nk // TILE, dtype=jnp.int32)
    hit = jnp.any(mask_rows[:, :, None] == ids[None, None, :], axis=1)
    live = jnp.broadcast_to(
        jnp.logical_not(hit)[:, None, :, None], (nq // TILE, TILE, nk // TILE, TILE)
    ).reshape(nq, nk)
    return (jnp.where(live, s, NEG), live)


def general(bank, queries, keys, labels, mask_tiles):
    qdev = queries.shape[0]
    bdev = bank.shape[0]
    total_bank = bdev * lax.axis_size("bank")
    total_query = qdev * lax.axis_size("batch")
    eta = 0.25 * total_bank / total_query
    mine = lax.axis_index("batch")
    first = lax.axis_index("bank") * (bdev // TILE)
    all_keys = lax.all_gather(keys, "batch", axis=0, tiled=True)
    key_rows = jnp.take(all_keys, labels, axis=0)
    pos = jnp.sum(queries.astype(jnp.float32) * key_rows.astype(jnp.float32), axis=1) / TAU
    own_mask = lax.dynamic_slice_in_dim(mask_tiles, mine * (qdev // TILE), qdev // TILE, 0)
    scores, live = masked_scores(queries, bank, own_mask, first)
    top = lax.pmax(jnp.max(scores, axis=1), "bank")
    part_sum = jnp.sum(jnp.where(live, jnp.exp(scores - top[:, None]), 0.0), axis=1)
    total = lax.psum(part_sum, "bank")
    high = jnp.maximum(top, pos)
    lse = high + jnp.log(total * jnp.exp(top - high) + jnp.exp(pos - high))
    loss = lse - pos
    probs = jnp.exp(scores - lse[:, None]).astype(jnp.bfloat16)
    neg_local = jnp.dot(probs, bank, preferred_element_type=jnp.float32)
    own_pull = jnp.einsum("qk,qd->kd", probs, queries, preferred_element_type=jnp.float32)
    neg = lax.psum(neg_local, "bank")
    query_grad = (neg + (jnp.exp(pos - lse) - 1.0)[:, None] * key_rows.astype(jnp.float32)) / TAU
    pull = lax.psum(own_pull.astype(jnp.bfloat16), "batch").astype(jnp.float32)
    fresh = bank.astype(jnp.float32) + eta * pull
    fresh = fresh * lax.rsqrt(jnp.mean(fresh * fresh, axis=1, keepdims=True) + EPS)
    return (fresh.astype(jnp.bfloat16), query_grad, loss)


def column(row):
    return jnp.transpose(jnp.broadcast_to(row, (TILE, TILE)))


def wide_column(row, width):
    return jnp.concatenate([column(row)] * (width // TILE), axis=1)


def step_kernel(
    n, eta, mask_hbm, bank_hbm, q_hbm, keys_hbm, labels_hbm,
    new_ref, grad_ref, loss_ref,
    mask_ref, bank_ref, q_ref, keys_ref, labels_ref,
    s_scr, p_scr, bankt_scr, bias_scr, keys_scr, stats_scr, qs_scr,
    stage_scr, rs_scr, pull_scr, pull_in_scr,
    in_sems, keys_sems, stats_send, stats_recv, rs_send, rs_recv, ag_send, ag_recv, pull_send, pull_recv,
):
    me = lax.axis_index("bank")
    mine = lax.axis_index("batch")
    other = 1 - mine
    bdev, width = bank_ref.shape
    qdev = q_ref.shape[0]
    tiles = bdev // TILE
    blocks = qdev // TILE
    listed = mask_ref.shape[1]
    first = me * tiles
    levels = n // 2
    z = me // 2
    x = lax.rem(me, 2)

    loads = [
        pltpu.make_async_copy(src, dst, in_sems.at[i])
        for i, (src, dst) in enumerate((
            (mask_hbm, mask_ref), (bank_hbm, bank_ref), (q_hbm, q_ref), (labels_hbm, labels_ref), (keys_hbm, keys_ref)))
    ]
    for load in loads:
        load.start()

    barrier = pltpu.get_barrier_semaphore()
    for d in range(1, n):
        pl.semaphore_signal(barrier, inc=1, device_id={"bank": lax.rem(me + d, n)}, device_id_type=MESH)
    pl.semaphore_signal(barrier, inc=1, device_id={"batch": other}, device_id_type=MESH)

    loads[0].wait()
    ids = first + lax.broadcasted_iota(jnp.int32, (tiles, TILE), 0)
    for b in range(blocks):
        hit = ids == mask_ref[mine * blocks + b, 0]
        for m in range(1, listed):
            hit = jnp.logical_or(hit, ids == mask_ref[mine * blocks + b, m])
        bias_scr[b] = jnp.where(hit, NEG, 0.0)

    loads[1].wait()
    for k in range(bdev // BCH):
        bankt_scr[:, k * BCH:(k + 1) * BCH] = jnp.transpose(bank_ref[k * BCH:(k + 1) * BCH, :])
    loads[2].wait()

    def keys_copy():
        return pltpu.make_async_remote_copy(
            src_ref=keys_hbm, dst_ref=keys_scr, send_sem=keys_sems.at[0], recv_sem=keys_sems.at[1],
            device_id={"batch": other}, device_id_type=MESH)

    def to_bank(peer, src, dst, send, recv):
        return pltpu.make_async_remote_copy(
            src_ref=src, dst_ref=dst, send_sem=send, recv_sem=recv,
            device_id={"bank": peer}, device_id_type=MESH)

    half = QCH // TILE
    scatter = []
    for step in range(levels):
        c = lax.rem(z + step + 1, levels)
        cols = pl.ds(pl.multiple_of(c * QCH, QCH), QCH)
        qc = q_ref[cols, :]
        top8 = jnp.full((8, QCH), FLOOR, jnp.float32)
        for k in range(bdev // BCH):
            s = lax.dot_general(bank_ref[k * BCH:(k + 1) * BCH, :], qc, (((1,), (1,)), ((), ())),
                                preferred_element_type=jnp.float32)
            for t in range(BCH // TILE):
                tile = k * (BCH // TILE) + t
                bias = jnp.concatenate([bias_scr[c * half + u, tile:tile + 1, :] for u in range(half)], axis=1)
                part = s[t * TILE:(t + 1) * TILE, :] * SCALE2 + bias
                s_scr[step % 2, tile * TILE:(tile + 1) * TILE, :] = part
                top8 = jnp.maximum(top8, jnp.max(part.reshape(TILE // 8, 8, QCH), axis=0))
        top = jnp.max(top8, axis=0, keepdims=True)
        sum8 = jnp.zeros((8, QCH), jnp.float32)
        for tile in range(tiles):
            rows = slice(tile * TILE, (tile + 1) * TILE)
            p = jnp.exp2(s_scr[step % 2, rows, :] - top)
            sum8 = sum8 + jnp.sum(p.reshape(TILE // 8, 8, QCH), axis=0)
            p_scr[rows, cols] = p.astype(jnp.bfloat16)
        total = jnp.sum(sum8, axis=0, keepdims=True)
        for u in range(half):
            b = c * half + u
            stats_scr[me, pl.ds(b, 1), :] = top[:, u * TILE:(u + 1) * TILE]
            stats_scr[me, pl.ds(8 + b, 1), :] = total[:, u * TILE:(u + 1) * TILE]
        if step == 0:
            pl.semaphore_wait(barrier, n)
            keys_copy().start()
        if step == levels - 1:
            stats = [to_bank(lax.rem(me + d, n), stats_scr.at[me], stats_scr.at[me], stats_send.at[d], stats_recv.at[d])
                     for d in range(1, n)]
            for copy in stats:
                copy.start()
        neg = jnp.dot(bankt_scr[...], p_scr[:, cols], preferred_element_type=jnp.float32).astype(jnp.bfloat16)
        for u in range(half):
            stage_scr[c * half + u] = neg[:, u * TILE:(u + 1) * TILE]
        for dx in range(2):
            if step == levels - 1 and dx == 0:
                continue
            j = 2 * step + dx
            peer = c * half + lax.rem(x + dx, 2)
            copy = to_bank(peer, stage_scr.at[peer], rs_scr.at[j], rs_send.at[j], rs_recv.at[j])
            copy.start()
            scatter.append((j, lax.rem(z + 2 * levels - step - 1, levels) * 2 + lax.rem(x + 2 - dx, 2), copy))

        if step == 1:
            loads[3].wait()
            loads[4].wait()
            own = pl.ds(pl.multiple_of(me * TILE, TILE), TILE)
            label_row = labels_ref[pl.ds(me, 1), :]
            row_ids = lax.broadcasted_iota(jnp.int32, (qdev, TILE), 0)

            def picked(table, start):
                hot = jnp.where(row_ids + start == label_row, 1.0, 0.0).astype(jnp.bfloat16)
                return lax.dot_general(hot, table, (((0,), (0,)), ((), ())), preferred_element_type=jnp.float32)

            key_rows = picked(keys_ref[...], mine * qdev)
            keys_copy().wait()
            key_rows = key_rows + picked(keys_scr[...], other * qdev)
            prod = q_ref[own, :].astype(jnp.float32) * key_rows
            own_pos = jnp.sum(jnp.transpose(prod), axis=0, keepdims=True) / TAU
            stats_scr[me, 16:24, :] = jnp.broadcast_to(own_pos, (8, TILE))

    for copy in stats:
        copy.wait()
    pos = jnp.concatenate([stats_scr[b, 16:17, :] for b in range(n)], axis=0) * LOG2E
    high = pos
    for b in range(n):
        high = jnp.maximum(high, stats_scr[b, 0:8, :])
    total = jnp.exp2(pos - high)
    for b in range(n):
        total = total + stats_scr[b, 8:16, :] * jnp.exp2(stats_scr[b, 0:8, :] - high)
    lse = high + jnp.log(total) * LOG2E
    loss_ref[...] = (lse - pos) * LN2
    alpha = jnp.exp2(stats_scr[me, 0:8, :] - lse)

    row_of = lax.broadcasted_iota(jnp.int32, (n, TILE), 0) == me

    def own_row(rows):
        return jnp.sum(jnp.where(row_of, rows, 0.0), axis=0, keepdims=True)

    own_lse = own_row(lse)
    factor = own_row(jnp.exp2(pos - lse) - 1.0)
    negs = stage_scr[me].astype(jnp.float32) * own_row(alpha)
    for j, sender, copy in scatter:
        copy.wait()
        scale = jnp.exp2(stats_scr[sender, pl.ds(me, 1), :] - own_lse)
        negs = negs + rs_scr[j].astype(jnp.float32) * scale
    grad = (jnp.transpose(negs) + wide_column(factor, width) * key_rows) / TAU
    grad_ref[me] = grad.astype(jnp.bfloat16)
    along = []
    for k in range(levels - 1):
        peer = lax.rem(z + k + 1, levels) * 2 + x
        along.append(to_bank(peer, grad_ref.at[me], grad_ref.at[me], ag_send.at[k], ag_recv.at[k]))
    across = z * 2 + 1 - x
    sides = [to_bank(across, grad_ref.at[me], grad_ref.at[me], ag_send.at[levels - 1], ag_recv.at[levels - 1])]
    for copy in along + sides:
        copy.start()

    for b in range(blocks):
        rows = slice(b * TILE, (b + 1) * TILE)
        qs_scr[rows, :] = (q_ref[rows, :].astype(jnp.float32) * wide_column(alpha[b:b + 1, :], width)).astype(jnp.bfloat16)
    exchange = []
    for k in range(bdev // BCH):
        rows = slice(k * BCH, (k + 1) * BCH)
        pull_scr[rows, :] = jnp.dot(p_scr[rows, :], qs_scr[...], preferred_element_type=jnp.float32).astype(jnp.bfloat16)
        copy = pltpu.make_async_remote_copy(
            src_ref=pull_scr.at[rows, :], dst_ref=pull_in_scr.at[rows, :],
            send_sem=pull_send.at[k], recv_sem=pull_recv.at[k],
            device_id={"batch": other}, device_id_type=MESH)
        copy.start()
        exchange.append(copy)

    for k in range(levels - 1):
        along[k].wait_recv()
        source = lax.rem(z + 2 * levels - k - 1, levels) * 2 + x
        j = levels + k
        copy = to_bank(across, grad_ref.at[source], grad_ref.at[source], ag_send.at[j], ag_recv.at[j])
        copy.start()
        sides.append(copy)

    for k in range(bdev // BCH):
        rows = slice(k * BCH, (k + 1) * BCH)
        exchange[k].wait()
        pull = pull_scr[rows, :].astype(jnp.float32) + pull_in_scr[rows, :].astype(jnp.float32)
        fresh = bank_ref[rows, :].astype(jnp.float32) + eta * pull
        fresh = fresh * lax.rsqrt(jnp.mean(fresh * fresh, axis=1, keepdims=True) + EPS)
        new_ref[rows, :] = fresh.astype(jnp.bfloat16)
    for copy in along:
        copy.wait_send()
    for copy in sides:
        copy.wait()


def fused(bank, queries, keys, labels, mask_tiles):
    n = lax.axis_size("bank")
    qdev, width = queries.shape
    bdev = bank.shape[0]
    eta = 0.25 * (bdev * n) / (qdev * lax.axis_size("batch"))
    vmem = pl.BlockSpec(memory_space=pltpu.VMEM)
    hbm = pl.BlockSpec(memory_space=pltpu.HBM)
    dma = pltpu.SemaphoreType.DMA
    new_bank, grad, loss = pl.pallas_call(
        functools.partial(step_kernel, n, eta),
        out_shape=(
            jax.ShapeDtypeStruct((bdev, width), jnp.bfloat16),
            jax.ShapeDtypeStruct((n, TILE, width), jnp.bfloat16),
            jax.ShapeDtypeStruct((n, TILE), jnp.float32),
        ),
        in_specs=[hbm] * 5,
        out_specs=(vmem, vmem, vmem),
        scratch_shapes=[
            pltpu.SMEM(mask_tiles.shape, jnp.int32),
            pltpu.VMEM((bdev, width), jnp.bfloat16),
            pltpu.VMEM((qdev, width), jnp.bfloat16),
            pltpu.VMEM((qdev, width), jnp.bfloat16),
            pltpu.VMEM((n, TILE), jnp.int32),
            pltpu.VMEM((2, bdev, QCH), jnp.float32),
            pltpu.VMEM((bdev, qdev), jnp.bfloat16),
            pltpu.VMEM((width, bdev), jnp.bfloat16),
            pltpu.VMEM((n, bdev // TILE, TILE), jnp.float32),
            pltpu.VMEM((qdev, width), jnp.bfloat16),
            pltpu.VMEM((n, 24, TILE), jnp.float32),
            pltpu.VMEM((qdev, width), jnp.bfloat16),
            pltpu.VMEM((n, width, TILE), jnp.bfloat16),
            pltpu.VMEM((n, width, TILE), jnp.bfloat16),
            pltpu.VMEM((bdev, width), jnp.bfloat16),
            pltpu.VMEM((bdev, width), jnp.bfloat16),
            dma((5,)),
            dma((2,)),
            dma((n,)), dma((n,)),
            dma((n,)), dma((n,)),
            dma((n,)), dma((n,)),
            dma((bdev // BCH,)), dma((bdev // BCH,)),
        ],
        compiler_params=pltpu.CompilerParams(
            collective_id=0, has_side_effects=True, vmem_limit_bytes=48 * 1024 * 1024
        ),
    )(mask_tiles, bank, queries, keys, labels.reshape(n, TILE))
    return (new_bank, grad.reshape(qdev, width).astype(jnp.float32), loss.reshape(qdev))


def on_device(bank, queries, keys, labels, mask_tiles):
    n = lax.axis_size("bank")
    fits = (
        n == 8
        and queries.shape[0] == n * TILE
        and bank.shape[0] % BCH == 0
        and lax.axis_size("batch") == 2
    )
    return (fused if fits else general)(bank, queries, keys, labels, mask_tiles)


def solution(mesh):
    return jax.shard_map(
        on_device,
        mesh=mesh,
        in_specs=(
            P(("parts", "bank"), None),
            P(("parts", "batch"), None),
            P(("parts", "batch"), None),
            P(("parts", "batch")),
            P("parts", None),
        ),
        out_specs=(P(("parts", "bank"), None), P(("parts", "batch"), None), P(("parts", "batch"))),
        check_vma=False,
    )
```

```python
import functools
import math

import jax
import jax.numpy as jnp
from jax import lax
from jax.experimental import pallas as pl
from jax.experimental.pallas import tpu as pltpu
from jax.sharding import PartitionSpec as P

TILE = 128


TAU = 0.12
NEG = -1e30
FLOOR = -1e29
EPS = 1e-06
LOG2E = math.log2(math.e)
LN2 = math.log(2.0)
SCALE2 = LOG2E / TAU
QCH = 256
BCH = 256
MESH = pl.DeviceIdType.MESH


def masked_scores(rows_q, rows_k, mask_rows, first):
    s = jnp.einsum("qd,kd->qk", rows_q, rows_k, preferred_element_type=jnp.float32) / TAU
    nq, nk = s.shape
    ids = first + jnp.arange(nk // TILE, dtype=jnp.int32)
    hit = jnp.any(mask_rows[:, :, None] == ids[None, None, :], axis=1)
    live = jnp.broadcast_to(
        jnp.logical_not(hit)[:, None, :, None], (nq // TILE, TILE, nk // TILE, TILE)
    ).reshape(nq, nk)
    return (jnp.where(live, s, NEG), live)


def general(bank, queries, keys, labels, mask_tiles):
    qdev = queries.shape[0]
    bdev = bank.shape[0]
    total_bank = bdev * lax.axis_size("bank")
    total_query = qdev * lax.axis_size("batch")
    eta = 0.25 * total_bank / total_query
    mine = lax.axis_index("batch")
    first = lax.axis_index("bank") * (bdev // TILE)
    all_keys = lax.all_gather(keys, "batch", axis=0, tiled=True)
    key_rows = jnp.take(all_keys, labels, axis=0)
    pos = jnp.sum(queries.astype(jnp.float32) * key_rows.astype(jnp.float32), axis=1) / TAU
    own_mask = lax.dynamic_slice_in_dim(mask_tiles, mine * (qdev // TILE), qdev // TILE, 0)
    scores, live = masked_scores(queries, bank, own_mask, first)
    top = lax.pmax(jnp.max(scores, axis=1), "bank")
    part_sum = jnp.sum(jnp.where(live, jnp.exp(scores - top[:, None]), 0.0), axis=1)
    total = lax.psum(part_sum, "bank")
    high = jnp.maximum(top, pos)
    lse = high + jnp.log(total * jnp.exp(top - high) + jnp.exp(pos - high))
    loss = lse - pos
    probs = jnp.exp(scores - lse[:, None]).astype(jnp.bfloat16)
    neg_local = jnp.dot(probs, bank, preferred_element_type=jnp.float32)
    own_pull = jnp.einsum("qk,qd->kd", probs, queries, preferred_element_type=jnp.float32)
    neg = lax.psum(neg_local, "bank")
    query_grad = (neg + (jnp.exp(pos - lse) - 1.0)[:, None] * key_rows.astype(jnp.float32)) / TAU
    pull = lax.psum(own_pull.astype(jnp.bfloat16), "batch").astype(jnp.float32)
    fresh = bank.astype(jnp.float32) + eta * pull
    fresh = fresh * lax.rsqrt(jnp.mean(fresh * fresh, axis=1, keepdims=True) + EPS)
    return (fresh.astype(jnp.bfloat16), query_grad, loss)


def column(row):
    return jnp.transpose(jnp.broadcast_to(row, (TILE, TILE)))


def wide_column(row, width):
    return jnp.concatenate([column(row)] * (width // TILE), axis=1)


def step_kernel(
    n, eta, mask_hbm, bank_hbm, q_hbm, keys_hbm, labels_hbm,
    new_ref, grad_ref, loss_ref,
    mask_ref, bank_ref, q_ref, keys_ref, labels_ref,
    s_scr, p_scr, bankt_scr, bias_scr, keys_scr, stats_scr, qs_scr,
    stage_scr, side_scr, top_out_scr, top_in_scr, pair_scr, rs_scr, pull_scr, pull_in_scr,
    in_sems, keys_sems, stats_send, stats_recv, side_send, side_recv, top_send, top_recv, rs_send, rs_recv, ag_send, ag_recv, pull_send, pull_recv,
):
    me = lax.axis_index("bank")
    mine = lax.axis_index("batch")
    other = 1 - mine
    bdev, width = bank_ref.shape
    qdev = q_ref.shape[0]
    tiles = bdev // TILE
    blocks = qdev // TILE
    listed = mask_ref.shape[1]
    first = me * tiles
    levels = n // 2
    z = me // 2
    x = lax.rem(me, 2)

    loads = [
        pltpu.make_async_copy(src, dst, in_sems.at[i])
        for i, (src, dst) in enumerate((
            (mask_hbm, mask_ref), (bank_hbm, bank_ref), (q_hbm, q_ref), (labels_hbm, labels_ref), (keys_hbm, keys_ref)))
    ]
    for load in loads:
        load.start()

    barrier = pltpu.get_barrier_semaphore()
    for d in range(1, n):
        pl.semaphore_signal(barrier, inc=1, device_id={"bank": lax.rem(me + d, n)}, device_id_type=MESH)
    pl.semaphore_signal(barrier, inc=1, device_id={"batch": other}, device_id_type=MESH)

    loads[0].wait()
    ids = first + lax.broadcasted_iota(jnp.int32, (tiles, TILE), 0)
    for b in range(blocks):
        hit = ids == mask_ref[mine * blocks + b, 0]
        for m in range(1, listed):
            hit = jnp.logical_or(hit, ids == mask_ref[mine * blocks + b, m])
        bias_scr[b] = jnp.where(hit, NEG, 0.0)

    loads[1].wait()
    for k in range(bdev // BCH):
        bankt_scr[:, k * BCH:(k + 1) * BCH] = jnp.transpose(bank_ref[k * BCH:(k + 1) * BCH, :])
    loads[2].wait()

    def keys_copy():
        return pltpu.make_async_remote_copy(
            src_ref=keys_hbm, dst_ref=keys_scr, send_sem=keys_sems.at[0], recv_sem=keys_sems.at[1],
            device_id={"batch": other}, device_id_type=MESH)

    def to_bank(peer, src, dst, send, recv):
        return pltpu.make_async_remote_copy(
            src_ref=src, dst_ref=dst, send_sem=send, recv_sem=recv,
            device_id={"bank": peer}, device_id_type=MESH)

    half = QCH // TILE
    across = z * 2 + 1 - x
    scatter = []
    sides = []
    kept = []

    def forward(step):
        for copy in sides[step]:
            copy.wait()
        came = top_in_scr[step, 0:1, :]
        both = jnp.maximum(kept[step], came)
        pair_scr[step] = (
            stage_scr[step, x].astype(jnp.float32) * jnp.exp2(kept[step] - both)
            + side_scr[step].astype(jnp.float32) * jnp.exp2(came - both)
        ).astype(jnp.bfloat16)
        copy = to_bank(lax.rem(z + step + 1, levels) * 2 + x, pair_scr.at[step], rs_scr.at[step],
                       rs_send.at[step], rs_recv.at[step])
        copy.start()
        scatter.append(copy)

    for step in range(levels):
        c = lax.rem(z + step + 1, levels)
        cols = pl.ds(pl.multiple_of(c * QCH, QCH), QCH)
        qc = q_ref[cols, :]
        top8 = jnp.full((8, QCH), FLOOR, jnp.float32)
        for k in range(bdev // BCH):
            s = lax.dot_general(bank_ref[k * BCH:(k + 1) * BCH, :], qc, (((1,), (1,)), ((), ())),
                                preferred_element_type=jnp.float32)
            for t in range(BCH // TILE):
                tile = k * (BCH // TILE) + t
                bias = jnp.concatenate([bias_scr[c * half + u, tile:tile + 1, :] for u in range(half)], axis=1)
                part = s[t * TILE:(t + 1) * TILE, :] * SCALE2 + bias
                s_scr[step % 2, tile * TILE:(tile + 1) * TILE, :] = part
                top8 = jnp.maximum(top8, jnp.max(part.reshape(TILE // 8, 8, QCH), axis=0))
        top = jnp.max(top8, axis=0, keepdims=True)
        sum8 = jnp.zeros((8, QCH), jnp.float32)
        for tile in range(tiles):
            rows = slice(tile * TILE, (tile + 1) * TILE)
            p = jnp.exp2(s_scr[step % 2, rows, :] - top)
            sum8 = sum8 + jnp.sum(p.reshape(TILE // 8, 8, QCH), axis=0)
            p_scr[rows, cols] = p.astype(jnp.bfloat16)
        total = jnp.sum(sum8, axis=0, keepdims=True)
        for u in range(half):
            b = c * half + u
            stats_scr[me, pl.ds(b, 1), :] = top[:, u * TILE:(u + 1) * TILE]
            stats_scr[me, pl.ds(8 + b, 1), :] = total[:, u * TILE:(u + 1) * TILE]
        if step == 0:
            pl.semaphore_wait(barrier, n)
            keys_copy().start()
        if step == levels - 1:
            stats = [to_bank(lax.rem(me + d, n), stats_scr.at[me], stats_scr.at[me], stats_send.at[d], stats_recv.at[d])
                     for d in range(1, n)]
            for copy in stats:
                copy.start()
        neg = jnp.dot(bankt_scr[...], p_scr[:, cols], preferred_element_type=jnp.float32).astype(jnp.bfloat16)
        for u in range(half):
            stage_scr[step, u] = neg[:, u * TILE:(u + 1) * TILE]
        halves = [top[:, u * TILE:(u + 1) * TILE] for u in range(half)]
        kept.append(jnp.where(x == 0, halves[0], halves[1]))
        top_out_scr[step] = jnp.broadcast_to(jnp.where(x == 0, halves[1], halves[0]), (8, TILE))
        pair = (
            to_bank(across, stage_scr.at[step, 1 - x], side_scr.at[step], side_send.at[step], side_recv.at[step]),
            to_bank(across, top_out_scr.at[step], top_in_scr.at[step], top_send.at[step], top_recv.at[step]),
        )
        for copy in pair:
            copy.start()
        sides.append(pair)
        if step > 0:
            forward(step - 1)

        if step == 1:
            loads[3].wait()
            loads[4].wait()
            own = pl.ds(pl.multiple_of(me * TILE, TILE), TILE)
            label_row = labels_ref[pl.ds(me, 1), :]
            row_ids = lax.broadcasted_iota(jnp.int32, (qdev, TILE), 0)

            def picked(table, start):
                hot = jnp.where(row_ids + start == label_row, 1.0, 0.0).astype(jnp.bfloat16)
                return lax.dot_general(hot, table, (((0,), (0,)), ((), ())), preferred_element_type=jnp.float32)

            key_rows = picked(keys_ref[...], mine * qdev)
            keys_copy().wait()
            key_rows = key_rows + picked(keys_scr[...], other * qdev)
            prod = q_ref[own, :].astype(jnp.float32) * key_rows
            own_pos = jnp.sum(jnp.transpose(prod), axis=0, keepdims=True) / TAU
            stats_scr[me, 16:24, :] = jnp.broadcast_to(own_pos, (8, TILE))

    for copy in stats:
        copy.wait()
    pos = jnp.concatenate([stats_scr[b, 16:17, :] for b in range(n)], axis=0) * LOG2E
    high = pos
    for b in range(n):
        high = jnp.maximum(high, stats_scr[b, 0:8, :])
    total = jnp.exp2(pos - high)
    for b in range(n):
        total = total + stats_scr[b, 8:16, :] * jnp.exp2(stats_scr[b, 0:8, :] - high)
    lse = high + jnp.log(total) * LOG2E
    loss_ref[...] = (lse - pos) * LN2
    alpha = jnp.exp2(stats_scr[me, 0:8, :] - lse)

    row_of = lax.broadcasted_iota(jnp.int32, (n, TILE), 0) == me

    def own_row(rows):
        return jnp.sum(jnp.where(row_of, rows, 0.0), axis=0, keepdims=True)

    own_lse = own_row(lse)
    factor = own_row(jnp.exp2(pos - lse) - 1.0)
    for copy in sides[levels - 1]:
        copy.wait()
    negs = (
        stage_scr[levels - 1, x].astype(jnp.float32) * jnp.exp2(kept[levels - 1] - own_lse)
        + side_scr[levels - 1].astype(jnp.float32) * jnp.exp2(top_in_scr[levels - 1, 0:1, :] - own_lse)
    )
    for step in range(levels - 1):
        scatter[step].wait()
        level = lax.rem(z + 2 * levels - step - 1, levels) * 2
        both = jnp.maximum(stats_scr[level, pl.ds(me, 1), :], stats_scr[level + 1, pl.ds(me, 1), :])
        negs = negs + rs_scr[step].astype(jnp.float32) * jnp.exp2(both - own_lse)
    grad = (jnp.transpose(negs) + wide_column(factor, width) * key_rows) / TAU
    grad_ref[me] = grad.astype(jnp.bfloat16)
    along = []
    for k in range(levels - 1):
        peer = lax.rem(z + k + 1, levels) * 2 + x
        along.append(to_bank(peer, grad_ref.at[me], grad_ref.at[me], ag_send.at[k], ag_recv.at[k]))
    sides = [to_bank(across, grad_ref.at[me], grad_ref.at[me], ag_send.at[levels - 1], ag_recv.at[levels - 1])]
    for copy in along + sides:
        copy.start()

    for b in range(blocks):
        rows = slice(b * TILE, (b + 1) * TILE)
        qs_scr[rows, :] = (q_ref[rows, :].astype(jnp.float32) * wide_column(alpha[b:b + 1, :], width)).astype(jnp.bfloat16)
    exchange = []
    for k in range(bdev // BCH):
        rows = slice(k * BCH, (k + 1) * BCH)
        pull_scr[rows, :] = jnp.dot(p_scr[rows, :], qs_scr[...], preferred_element_type=jnp.float32).astype(jnp.bfloat16)
        copy = pltpu.make_async_remote_copy(
            src_ref=pull_scr.at[rows, :], dst_ref=pull_in_scr.at[rows, :],
            send_sem=pull_send.at[k], recv_sem=pull_recv.at[k],
            device_id={"batch": other}, device_id_type=MESH)
        copy.start()
        exchange.append(copy)

    for k in range(levels - 1):
        along[k].wait_recv()
        source = lax.rem(z + 2 * levels - k - 1, levels) * 2 + x
        j = levels + k
        copy = to_bank(across, grad_ref.at[source], grad_ref.at[source], ag_send.at[j], ag_recv.at[j])
        copy.start()
        sides.append(copy)

    for k in range(bdev // BCH):
        rows = slice(k * BCH, (k + 1) * BCH)
        exchange[k].wait()
        pull = pull_scr[rows, :].astype(jnp.float32) + pull_in_scr[rows, :].astype(jnp.float32)
        fresh = bank_ref[rows, :].astype(jnp.float32) + eta * pull
        fresh = fresh * lax.rsqrt(jnp.mean(fresh * fresh, axis=1, keepdims=True) + EPS)
        new_ref[rows, :] = fresh.astype(jnp.bfloat16)
    for copy in along:
        copy.wait_send()
    for copy in sides:
        copy.wait()


def fused(bank, queries, keys, labels, mask_tiles):
    n = lax.axis_size("bank")
    qdev, width = queries.shape
    bdev = bank.shape[0]
    eta = 0.25 * (bdev * n) / (qdev * lax.axis_size("batch"))
    vmem = pl.BlockSpec(memory_space=pltpu.VMEM)
    hbm = pl.BlockSpec(memory_space=pltpu.HBM)
    dma = pltpu.SemaphoreType.DMA
    new_bank, grad, loss = pl.pallas_call(
        functools.partial(step_kernel, n, eta),
        out_shape=(
            jax.ShapeDtypeStruct((bdev, width), jnp.bfloat16),
            jax.ShapeDtypeStruct((n, TILE, width), jnp.bfloat16),
            jax.ShapeDtypeStruct((n, TILE), jnp.float32),
        ),
        in_specs=[hbm] * 5,
        out_specs=(vmem, vmem, vmem),
        scratch_shapes=[
            pltpu.SMEM(mask_tiles.shape, jnp.int32),
            pltpu.VMEM((bdev, width), jnp.bfloat16),
            pltpu.VMEM((qdev, width), jnp.bfloat16),
            pltpu.VMEM((qdev, width), jnp.bfloat16),
            pltpu.VMEM((n, TILE), jnp.int32),
            pltpu.VMEM((2, bdev, QCH), jnp.float32),
            pltpu.VMEM((bdev, qdev), jnp.bfloat16),
            pltpu.VMEM((width, bdev), jnp.bfloat16),
            pltpu.VMEM((n, bdev // TILE, TILE), jnp.float32),
            pltpu.VMEM((qdev, width), jnp.bfloat16),
            pltpu.VMEM((n, 24, TILE), jnp.float32),
            pltpu.VMEM((qdev, width), jnp.bfloat16),
            pltpu.VMEM((n // 2, 2, width, TILE), jnp.bfloat16),
            pltpu.VMEM((n // 2, width, TILE), jnp.bfloat16),
            pltpu.VMEM((n // 2, 8, TILE), jnp.float32),
            pltpu.VMEM((n // 2, 8, TILE), jnp.float32),
            pltpu.VMEM((n // 2, width, TILE), jnp.bfloat16),
            pltpu.VMEM((n // 2, width, TILE), jnp.bfloat16),
            pltpu.VMEM((bdev, width), jnp.bfloat16),
            pltpu.VMEM((bdev, width), jnp.bfloat16),
            dma((5,)),
            dma((2,)),
            dma((n,)), dma((n,)),
            dma((n // 2,)), dma((n // 2,)),
            dma((n // 2,)), dma((n // 2,)),
            dma((n,)), dma((n,)),
            dma((n,)), dma((n,)),
            dma((bdev // BCH,)), dma((bdev // BCH,)),
        ],
        compiler_params=pltpu.CompilerParams(
            collective_id=0, has_side_effects=True, vmem_limit_bytes=60 * 1024 * 1024
        ),
    )(mask_tiles, bank, queries, keys, labels.reshape(n, TILE))
    return (new_bank, grad.reshape(qdev, width).astype(jnp.float32), loss.reshape(qdev))


def on_device(bank, queries, keys, labels, mask_tiles):
    n = lax.axis_size("bank")
    fits = (
        n == 8
        and queries.shape[0] == n * TILE
        and bank.shape[0] % BCH == 0
        and lax.axis_size("batch") == 2
    )
    return (fused if fits else general)(bank, queries, keys, labels, mask_tiles)


def solution(mesh):
    return jax.shard_map(
        on_device,
        mesh=mesh,
        in_specs=(
            P(("parts", "bank"), None),
            P(("parts", "batch"), None),
            P(("parts", "batch"), None),
            P(("parts", "batch")),
            P("parts", None),
        ),
        out_specs=(P(("parts", "bank"), None), P(("parts", "batch"), None), P(("parts", "batch"))),
        check_vma=False,
    )
```

```python
import functools
import math

import jax
import jax.numpy as jnp
from jax import lax
from jax.experimental import pallas as pl
from jax.experimental.pallas import tpu as pltpu
from jax.sharding import PartitionSpec as P

TILE = 128


TAU = 0.12
NEG = -1e30
FLOOR = -1e29
EPS = 1e-06
LOG2E = math.log2(math.e)
LN2 = math.log(2.0)
SCALE2 = LOG2E / TAU
QCH = 256
BCH = 256
MESH = pl.DeviceIdType.MESH


def masked_scores(rows_q, rows_k, mask_rows, first):
    s = jnp.einsum("qd,kd->qk", rows_q, rows_k, preferred_element_type=jnp.float32) / TAU
    nq, nk = s.shape
    ids = first + jnp.arange(nk // TILE, dtype=jnp.int32)
    hit = jnp.any(mask_rows[:, :, None] == ids[None, None, :], axis=1)
    live = jnp.broadcast_to(
        jnp.logical_not(hit)[:, None, :, None], (nq // TILE, TILE, nk // TILE, TILE)
    ).reshape(nq, nk)
    return (jnp.where(live, s, NEG), live)


def general(bank, queries, keys, labels, mask_tiles):
    qdev = queries.shape[0]
    bdev = bank.shape[0]
    total_bank = bdev * lax.axis_size("bank")
    total_query = qdev * lax.axis_size("batch")
    eta = 0.25 * total_bank / total_query
    mine = lax.axis_index("batch")
    first = lax.axis_index("bank") * (bdev // TILE)
    all_keys = lax.all_gather(keys, "batch", axis=0, tiled=True)
    key_rows = jnp.take(all_keys, labels, axis=0)
    pos = jnp.sum(queries.astype(jnp.float32) * key_rows.astype(jnp.float32), axis=1) / TAU
    own_mask = lax.dynamic_slice_in_dim(mask_tiles, mine * (qdev // TILE), qdev // TILE, 0)
    scores, live = masked_scores(queries, bank, own_mask, first)
    top = lax.pmax(jnp.max(scores, axis=1), "bank")
    part_sum = jnp.sum(jnp.where(live, jnp.exp(scores - top[:, None]), 0.0), axis=1)
    total = lax.psum(part_sum, "bank")
    high = jnp.maximum(top, pos)
    lse = high + jnp.log(total * jnp.exp(top - high) + jnp.exp(pos - high))
    loss = lse - pos
    probs = jnp.exp(scores - lse[:, None]).astype(jnp.bfloat16)
    neg_local = jnp.dot(probs, bank, preferred_element_type=jnp.float32)
    own_pull = jnp.einsum("qk,qd->kd", probs, queries, preferred_element_type=jnp.float32)
    neg = lax.psum(neg_local, "bank")
    query_grad = (neg + (jnp.exp(pos - lse) - 1.0)[:, None] * key_rows.astype(jnp.float32)) / TAU
    pull = lax.psum(own_pull.astype(jnp.bfloat16), "batch").astype(jnp.float32)
    fresh = bank.astype(jnp.float32) + eta * pull
    fresh = fresh * lax.rsqrt(jnp.mean(fresh * fresh, axis=1, keepdims=True) + EPS)
    return (fresh.astype(jnp.bfloat16), query_grad, loss)


def column(row):
    return jnp.transpose(jnp.broadcast_to(row, (TILE, TILE)))


def wide_column(row, width):
    return jnp.concatenate([column(row)] * (width // TILE), axis=1)


def step_kernel(
    n, eta, mask_hbm, bank_hbm, q_hbm, keys_hbm, labels_hbm,
    new_ref, grad_ref, loss_ref,
    mask_ref, bank_ref, q_ref, keys_ref, labels_ref,
    s_scr, p_scr, bankt_scr, bias_scr, keys_scr, stats_scr, qs_scr,
    stage_scr, side_scr, top_out_scr, top_in_scr, pair_scr, rs_scr, pull_scr, pull_in_scr,
    in_sems, keys_sems, stats_send, stats_recv, side_send, side_recv, top_send, top_recv, rs_send, rs_recv, ag_send, ag_recv, pull_send, pull_recv,
):
    me = lax.axis_index("bank")
    mine = lax.axis_index("batch")
    other = 1 - mine
    bdev, width = bank_ref.shape
    qdev = q_ref.shape[0]
    tiles = bdev // TILE
    blocks = qdev // TILE
    listed = mask_ref.shape[1]
    first = me * tiles
    levels = n // 2
    z = me // 2
    x = lax.rem(me, 2)

    loads = [
        pltpu.make_async_copy(src, dst, in_sems.at[i])
        for i, (src, dst) in enumerate((
            (mask_hbm, mask_ref), (bank_hbm, bank_ref), (q_hbm, q_ref), (labels_hbm, labels_ref), (keys_hbm, keys_ref)))
    ]
    for load in loads:
        load.start()

    barrier = pltpu.get_barrier_semaphore()
    for d in range(1, n):
        pl.semaphore_signal(barrier, inc=1, device_id={"bank": lax.rem(me + d, n)}, device_id_type=MESH)
    pl.semaphore_signal(barrier, inc=1, device_id={"batch": other}, device_id_type=MESH)

    loads[0].wait()
    ids = first + lax.broadcasted_iota(jnp.int32, (tiles, TILE), 0)
    for b in range(blocks):
        hit = ids == mask_ref[mine * blocks + b, 0]
        for m in range(1, listed):
            hit = jnp.logical_or(hit, ids == mask_ref[mine * blocks + b, m])
        bias_scr[b] = jnp.where(hit, NEG, 0.0)

    loads[1].wait()
    for k in range(bdev // BCH):
        bankt_scr[:, k * BCH:(k + 1) * BCH] = jnp.transpose(bank_ref[k * BCH:(k + 1) * BCH, :])
    loads[2].wait()

    def keys_copy():
        return pltpu.make_async_remote_copy(
            src_ref=keys_hbm, dst_ref=keys_scr, send_sem=keys_sems.at[0], recv_sem=keys_sems.at[1],
            device_id={"batch": other}, device_id_type=MESH)

    def to_bank(peer, src, dst, send, recv):
        return pltpu.make_async_remote_copy(
            src_ref=src, dst_ref=dst, send_sem=send, recv_sem=recv,
            device_id={"bank": peer}, device_id_type=MESH)

    half = QCH // TILE
    across = z * 2 + 1 - x
    scatter = []
    sides = []
    kept = []

    def forward(step):
        for copy in sides[step]:
            copy.wait()
        came = top_in_scr[step, 0:1, :]
        both = jnp.maximum(kept[step], came)
        pair_scr[step] = (
            stage_scr[step, x].astype(jnp.float32) * jnp.exp2(kept[step] - both)
            + side_scr[step].astype(jnp.float32) * jnp.exp2(came - both)
        ).astype(jnp.bfloat16)
        copy = to_bank(lax.rem(z + step + 1, levels) * 2 + x, pair_scr.at[step], rs_scr.at[step],
                       rs_send.at[step], rs_recv.at[step])
        copy.start()
        scatter.append(copy)

    for step in range(levels):
        c = lax.rem(z + step + 1, levels)
        cols = pl.ds(pl.multiple_of(c * QCH, QCH), QCH)
        qc = q_ref[cols, :]
        top8 = jnp.full((8, QCH), FLOOR, jnp.float32)
        for k in range(bdev // BCH):
            s = lax.dot_general(bank_ref[k * BCH:(k + 1) * BCH, :], qc, (((1,), (1,)), ((), ())),
                                preferred_element_type=jnp.float32)
            for t in range(BCH // TILE):
                tile = k * (BCH // TILE) + t
                bias = jnp.concatenate([bias_scr[c * half + u, tile:tile + 1, :] for u in range(half)], axis=1)
                part = s[t * TILE:(t + 1) * TILE, :] * SCALE2 + bias
                s_scr[step % 2, tile * TILE:(tile + 1) * TILE, :] = part
                top8 = jnp.maximum(top8, jnp.max(part.reshape(TILE // 8, 8, QCH), axis=0))
        top = jnp.max(top8, axis=0, keepdims=True)
        sum8 = jnp.zeros((8, QCH), jnp.float32)
        for tile in range(tiles):
            rows = slice(tile * TILE, (tile + 1) * TILE)
            p = jnp.exp2(s_scr[step % 2, rows, :] - top)
            sum8 = sum8 + jnp.sum(p.reshape(TILE // 8, 8, QCH), axis=0)
            p_scr[rows, cols] = p.astype(jnp.bfloat16)
        total = jnp.sum(sum8, axis=0, keepdims=True)
        for u in range(half):
            b = c * half + u
            stats_scr[me, pl.ds(b, 1), :] = top[:, u * TILE:(u + 1) * TILE]
            stats_scr[me, pl.ds(8 + b, 1), :] = total[:, u * TILE:(u + 1) * TILE]
        if step == 0:
            pl.semaphore_wait(barrier, n)
            keys_copy().start()
        if step == levels - 1:
            stats = [to_bank(lax.rem(me + d, n), stats_scr.at[me], stats_scr.at[me], stats_send.at[d], stats_recv.at[d])
                     for d in range(1, n)]
            for copy in stats:
                copy.start()
        neg = jnp.dot(bankt_scr[...], p_scr[:, cols], preferred_element_type=jnp.float32).astype(jnp.bfloat16)
        for u in range(half):
            stage_scr[step, u] = neg[:, u * TILE:(u + 1) * TILE]
        halves = [top[:, u * TILE:(u + 1) * TILE] for u in range(half)]
        kept.append(jnp.where(x == 0, halves[0], halves[1]))
        top_out_scr[step] = jnp.broadcast_to(jnp.where(x == 0, halves[1], halves[0]), (8, TILE))
        pair = (
            to_bank(across, stage_scr.at[step, 1 - x], side_scr.at[step], side_send.at[step], side_recv.at[step]),
            to_bank(across, top_out_scr.at[step], top_in_scr.at[step], top_send.at[step], top_recv.at[step]),
        )
        for copy in pair:
            copy.start()
        sides.append(pair)
        if step > 0:
            forward(step - 1)

        if step == 1:
            loads[3].wait()
            loads[4].wait()
            own = pl.ds(pl.multiple_of(me * TILE, TILE), TILE)
            label_row = labels_ref[pl.ds(me, 1), :]
            row_ids = lax.broadcasted_iota(jnp.int32, (qdev, TILE), 0)

            def picked(table, start):
                hot = jnp.where(row_ids + start == label_row, 1.0, 0.0).astype(jnp.bfloat16)
                return lax.dot_general(hot, table, (((0,), (0,)), ((), ())), preferred_element_type=jnp.float32)

            key_rows = picked(keys_ref[...], mine * qdev)
            keys_copy().wait()
            key_rows = key_rows + picked(keys_scr[...], other * qdev)
            prod = q_ref[own, :].astype(jnp.float32) * key_rows
            own_pos = jnp.sum(jnp.transpose(prod), axis=0, keepdims=True) / TAU
            stats_scr[me, 16:24, :] = jnp.broadcast_to(own_pos, (8, TILE))

    for copy in stats:
        copy.wait()
    pos = jnp.concatenate([stats_scr[b, 16:17, :] for b in range(n)], axis=0) * LOG2E
    high = pos
    for b in range(n):
        high = jnp.maximum(high, stats_scr[b, 0:8, :])
    total = jnp.exp2(pos - high)
    for b in range(n):
        total = total + stats_scr[b, 8:16, :] * jnp.exp2(stats_scr[b, 0:8, :] - high)
    lse = high + jnp.log(total) * LOG2E
    loss_ref[...] = (lse - pos) * LN2
    alpha = jnp.exp2(stats_scr[me, 0:8, :] - lse)

    row_of = lax.broadcasted_iota(jnp.int32, (n, TILE), 0) == me

    def own_row(rows):
        return jnp.sum(jnp.where(row_of, rows, 0.0), axis=0, keepdims=True)

    own_lse = own_row(lse)
    factor = own_row(jnp.exp2(pos - lse) - 1.0)
    for copy in sides[levels - 1]:
        copy.wait()
    negs = (
        stage_scr[levels - 1, x].astype(jnp.float32) * jnp.exp2(kept[levels - 1] - own_lse)
        + side_scr[levels - 1].astype(jnp.float32) * jnp.exp2(top_in_scr[levels - 1, 0:1, :] - own_lse)
    )
    for step in range(levels - 1):
        scatter[step].wait()
        level = lax.rem(z + 2 * levels - step - 1, levels) * 2
        both = jnp.maximum(stats_scr[level, pl.ds(me, 1), :], stats_scr[level + 1, pl.ds(me, 1), :])
        negs = negs + rs_scr[step].astype(jnp.float32) * jnp.exp2(both - own_lse)
    grad = (jnp.transpose(negs) + wide_column(factor, width) * key_rows) / TAU
    grad_ref[me] = grad.astype(jnp.bfloat16)
    along = []
    for k in range(levels - 1):
        peer = lax.rem(z + k + 1, levels) * 2 + x
        along.append(to_bank(peer, grad_ref.at[me], grad_ref.at[me], ag_send.at[k], ag_recv.at[k]))
    sides = [to_bank(across, grad_ref.at[me], grad_ref.at[me], ag_send.at[levels - 1], ag_recv.at[levels - 1])]
    for copy in along + sides:
        copy.start()

    for b in range(blocks):
        rows = slice(b * TILE, (b + 1) * TILE)
        qs_scr[rows, :] = (q_ref[rows, :].astype(jnp.float32) * wide_column(alpha[b:b + 1, :], width)).astype(jnp.bfloat16)
    exchange = []
    for k in range(bdev // BCH):
        rows = slice(k * BCH, (k + 1) * BCH)
        pull_scr[rows, :] = jnp.dot(p_scr[rows, :], qs_scr[...], preferred_element_type=jnp.float32).astype(jnp.bfloat16)
        copy = pltpu.make_async_remote_copy(
            src_ref=pull_scr.at[rows, :], dst_ref=pull_in_scr.at[rows, :],
            send_sem=pull_send.at[k], recv_sem=pull_recv.at[k],
            device_id={"batch": other}, device_id_type=MESH)
        copy.start()
        exchange.append(copy)

    for k in range(levels - 1):
        along[k].wait_recv()
        source = lax.rem(z + 2 * levels - k - 1, levels) * 2 + x
        j = levels + k
        copy = to_bank(across, grad_ref.at[source], grad_ref.at[source], ag_send.at[j], ag_recv.at[j])
        copy.start()
        sides.append(copy)

    for k in range(bdev // BCH):
        rows = slice(k * BCH, (k + 1) * BCH)
        exchange[k].wait()
        pull = pull_scr[rows, :].astype(jnp.float32) + pull_in_scr[rows, :].astype(jnp.float32)
        fresh = bank_ref[rows, :].astype(jnp.float32) + eta * pull
        fresh = fresh * lax.rsqrt(jnp.mean(fresh * fresh, axis=1, keepdims=True) + EPS)
        new_ref[rows, :] = fresh.astype(jnp.bfloat16)
    for copy in along:
        copy.wait_send()
    for copy in sides:
        copy.wait()


def fused(bank, queries, keys, labels, mask_tiles):
    n = lax.axis_size("bank")
    qdev, width = queries.shape
    bdev = bank.shape[0]
    eta = 0.25 * (bdev * n) / (qdev * lax.axis_size("batch"))
    vmem = pl.BlockSpec(memory_space=pltpu.VMEM)
    hbm = pl.BlockSpec(memory_space=pltpu.HBM)
    dma = pltpu.SemaphoreType.DMA
    new_bank, grad, loss = pl.pallas_call(
        functools.partial(step_kernel, n, eta),
        out_shape=(
            jax.ShapeDtypeStruct((bdev, width), jnp.bfloat16),
            jax.ShapeDtypeStruct((n, TILE, width), jnp.bfloat16),
            jax.ShapeDtypeStruct((n, TILE), jnp.float32),
        ),
        in_specs=[hbm] * 5,
        out_specs=(vmem, vmem, vmem),
        scratch_shapes=[
            pltpu.SMEM(mask_tiles.shape, jnp.int32),
            pltpu.VMEM((bdev, width), jnp.bfloat16),
            pltpu.VMEM((qdev, width), jnp.bfloat16),
            pltpu.VMEM((qdev, width), jnp.bfloat16),
            pltpu.VMEM((n, TILE), jnp.int32),
            pltpu.VMEM((2, bdev, QCH), jnp.float32),
            pltpu.VMEM((bdev, qdev), jnp.bfloat16),
            pltpu.VMEM((width, bdev), jnp.bfloat16),
            pltpu.VMEM((n, bdev // TILE, TILE), jnp.float32),
            pltpu.VMEM((qdev, width), jnp.bfloat16),
            pltpu.VMEM((n, 24, TILE), jnp.float32),
            pltpu.VMEM((qdev, width), jnp.bfloat16),
            pltpu.VMEM((n // 2, 2, width, TILE), jnp.bfloat16),
            pltpu.VMEM((n // 2, width, TILE), jnp.bfloat16),
            pltpu.VMEM((n // 2, 8, TILE), jnp.float32),
            pltpu.VMEM((n // 2, 8, TILE), jnp.float32),
            pltpu.VMEM((n // 2, width, TILE), jnp.bfloat16),
            pltpu.VMEM((n // 2, width, TILE), jnp.bfloat16),
            pltpu.VMEM((bdev, width), jnp.bfloat16),
            pltpu.VMEM((bdev, width), jnp.bfloat16),
            dma((5,)),
            dma((2,)),
            dma((n,)), dma((n,)),
            dma((n // 2,)), dma((n // 2,)),
            dma((n // 2,)), dma((n // 2,)),
            dma((n,)), dma((n,)),
            dma((n,)), dma((n,)),
            dma((bdev // BCH,)), dma((bdev // BCH,)),
        ],
        compiler_params=pltpu.CompilerParams(
            collective_id=0, has_side_effects=True, vmem_limit_bytes=60 * 1024 * 1024
        ),
    )(mask_tiles, bank, queries, keys, labels.reshape(n, TILE))
    new_bank, query_grad, loss = finish(new_bank, grad.reshape(qdev, width), loss)
    return (new_bank, query_grad, loss.reshape(qdev))


def finish_kernel(bank_in, grad_in, loss_in, bank_out, grad_out, loss_out):
    bank_out[...] = bank_in[...]
    grad_out[...] = grad_in[...].astype(jnp.float32)
    loss_out[...] = loss_in[...]


def finish(new_bank, grad, loss):
    bdev, width = new_bank.shape
    qdev = grad.shape[0]
    steps = 2
    whole = pl.BlockSpec(loss.shape, lambda i: (0, 0))
    specs = (
        pl.BlockSpec((bdev // steps, width), lambda i: (i, 0)),
        pl.BlockSpec((qdev // steps, width), lambda i: (i, 0)),
        whole,
    )
    return pl.pallas_call(
        finish_kernel,
        grid=(steps,),
        out_shape=(
            jax.ShapeDtypeStruct((bdev, width), jnp.bfloat16),
            jax.ShapeDtypeStruct((qdev, width), jnp.float32),
            jax.ShapeDtypeStruct(loss.shape, jnp.float32),
        ),
        in_specs=list(specs),
        out_specs=specs,
    )(new_bank, grad, loss)


def on_device(bank, queries, keys, labels, mask_tiles):
    n = lax.axis_size("bank")
    fits = (
        n == 8
        and queries.shape[0] == n * TILE
        and bank.shape[0] % BCH == 0
        and lax.axis_size("batch") == 2
    )
    return (fused if fits else general)(bank, queries, keys, labels, mask_tiles)


def solution(mesh):
    return jax.shard_map(
        on_device,
        mesh=mesh,
        in_specs=(
            P(("parts", "bank"), None),
            P(("parts", "batch"), None),
            P(("parts", "batch"), None),
            P(("parts", "batch")),
            P("parts", None),
        ),
        out_specs=(P(("parts", "bank"), None), P(("parts", "batch"), None), P(("parts", "batch"))),
        check_vma=False,
    )
```
